32 devices in a mesh: grp: 2 (over y), comp: 4 (over z), space: 4 (over x, core).
Axes of the slice: x: 2, y: 2, z: 4, core: 2. Of those that a mesh axis runs over, the one named last changes fastest.
Arguments:
- spectrum: float32 [2304, 4096], P('comp', ('grp', 'space')), parts along dimension 1, may hold values from -6 to 6
- wave_speed: float32 [36], replicated, may hold values from 0.25 to 2
- current_east: float32 [4096], P(('grp', 'space')), parts along dimension 0, may hold values from -3 to 3
- current_north: float32 [4096], P(('grp', 'space')), parts along dimension 0, may hold values from -3 to 3
- substeps: int32 [2304], replicated, may hold values from 1 to 4, as said below
- neighbours: int32 [4, 4096], P(None, ('grp', 'space')), parts along dimension 1, may hold values from 0 to 767, as said below
- blocks: bfloat16 [64, 64, 64], replicated, may hold values from -0.75 to 0.75
- quad_index: int32 [4, 64], replicated, may hold values from 0 to 35
- strength: float32 [64], replicated, may hold values from -1 to 1
Outputs:
- spectrum_out: float32 [2304, 4096], P('comp', ('grp', 'space')), parts along dimension 1
The draws below stay inside these ranges and needn't reach their ends.
There are 2 independent parts, one for each index of `grp`. The reference program is written for one: setup_inputs(seed, part) draws one part's arguments, and reference() takes and returns one part's arrays. A program takes and returns all parts, laid end to end along the dimension named above; an argument that names none is the same for every part. Nothing has to cross between parts.
Inputs may be any that keep to these rules, and one draw needn't show every extreme that they name: `substeps`: component 0 takes 4. `neighbours`: the entry of row r for the slab's point q (counted within its slab) is q + 128 + o, with -128 <= o <= -1 for rows 0 and 2 and 1 <= o <= 128 for rows 1 and 3.
All inputs are finite; a program needn't handle non-finite values.
Results may differ from the reference program's by a relative error of at most 0.00031.
Values sent between devices are 32-bit elements; how exact they have to be, the bound alone decides.
A program may use at most 64 MiB of HBM per device.

```python
import math
import jax
import jax.numpy as jnp
from jax import lax

NF = 36
ND = 64
NBLK = 64
SUB = 4
HALO = 128
STEPS = 1
K = 2304
PTS_SLAB = 512
PTS = 2048


def draw_substeps(key, part):
    components = jnp.arange(NF * ND, dtype=jnp.int32)
    frequency = components // ND
    jitter = jax.random.randint(key, (NF * ND,), -1, 1, dtype=jnp.int32)
    counts = SUB - frequency * SUB // NF + jitter
    counts = jnp.clip(counts, 1, SUB)
    return counts.at[0].set(SUB).astype(jnp.int32)


def draw_neighbours(key, part):
    offsets = jax.random.randint(key, (4, PTS), 1, HALO + 1, dtype=jnp.int32)
    direction_sign = jnp.array([-1, 1, -1, 1], dtype=jnp.int32)[:, None]
    position = (jnp.arange(PTS, dtype=jnp.int32) % PTS_SLAB)[None, :]
    row_number = jnp.arange(4, dtype=jnp.int32)[:, None]
    extended = position + HALO + direction_sign * offsets
    extended = jnp.where((row_number == 0) & (position == 0), 0, extended)
    extended = jnp.where((row_number == 1) & (position == PTS_SLAB - 1), PTS_SLAB + 2 * HALO - 1, extended)
    return extended.astype(jnp.int32)


def draw_quad_index(key, part):
    table = jax.random.randint(key, (4, NBLK), 0, NF, dtype=jnp.int32)
    table = table.at[:, 0].set(0)
    table = table.at[:, 1].set(NF - 1)
    return table.astype(jnp.int32)


def shard_levels(own_key, extent, shards, least, high):
    level, own = 1.0, jax.random.fold_in(own_key, 6)
    for dim, shards_of in shards:
        steps = jnp.exp(jax.random.uniform(jax.random.fold_in(own, dim), (shards_of,), jnp.float32, least / len(shards), high / len(shards)))
        level = level * jnp.repeat(steps, extent[dim] // shards_of).reshape([-1 if axis == dim else 1 for axis in range(len(extent))])
    return level


def scatter_about(rng, extent, deviation, bound, cuts=(), held_as=jnp.bfloat16):
    result = deviation * jax.random.normal(rng, extent, jnp.float32)
    if cuts:
        result = result * shard_levels(rng, extent, cuts, -0.22, 0.18)
    return jnp.clip(result, -bound, bound).astype(held_as)


def setup_inputs(seed: int = 0, part: int = 0) -> dict:
    key_of = jax.random.split(jax.random.key(seed), 10)
    part_splits = jax.random.split(jax.random.fold_in(key_of[9], part), 10)
    return {
        "spectrum": scatter_about(part_splits[0], (K, PTS), 1.0, 6.0, ((0, 4), (1, 4)), jnp.float32),
        "wave_speed": jnp.clip(jnp.exp(jax.random.uniform(key_of[1], (NF,), jnp.float32, math.log(0.25), math.log(2.0))), 0.25, 2.0),
        "current_east": scatter_about(part_splits[2], (PTS,), 0.5, 3.0, ((0, 4),), jnp.float32),
        "current_north": scatter_about(part_splits[3], (PTS,), 0.5, 3.0, ((0, 4),), jnp.float32),
        "substeps": draw_substeps(jax.random.fold_in(key_of[9], 71), part),
        "neighbours": draw_neighbours(jax.random.fold_in(jax.random.fold_in(key_of[9], part), 71), part),
        "blocks": scatter_about(key_of[6], (NBLK, ND, ND), ND ** -0.5, 0.75),
        "quad_index": draw_quad_index(jax.random.fold_in(key_of[9], 71), part),
        "strength": jnp.clip(jax.random.uniform(key_of[8], (NBLK,), jnp.float32, -1.0, 1.0), -1.0, 1.0),
    }


courant_scale = 0.4
courant_limit = 0.45
source_step = 0.1


def reference(spectrum, wave_speed, current_east, current_north, substeps, neighbours, blocks, quad_index, strength):
    global_index = (jnp.arange(PTS, dtype=jnp.int32) // PTS_SLAB) * PTS_SLAB + neighbours
    angles = (jnp.arange(ND, dtype=jnp.float32) + 0.5) * (2.0 * math.pi / ND)

    def per_frequency(members):
        values, speed_value, counts = members
        divisor = counts.astype(jnp.float32)[:, None]
        along_x = jnp.clip(((speed_value * jnp.cos(angles))[:, None] + current_east[None, :]) * courant_scale / divisor, -courant_limit, courant_limit)
        along_y = jnp.clip(((speed_value * jnp.sin(angles))[:, None] + current_north[None, :]) * courant_scale / divisor, -courant_limit, courant_limit)
        pos_x = jnp.maximum(along_x, 0.0)
        neg_x = jnp.minimum(along_x, 0.0)
        pos_y = jnp.maximum(along_y, 0.0)
        neg_y = jnp.minimum(along_y, 0.0)
        for repeat in range(SUB):
            padded = jnp.pad(values, ((0, 0), (HALO, HALO)))
            west_value = padded[:, global_index[0]]
            east_value = padded[:, global_index[1]]
            south_value = padded[:, global_index[2]]
            north_value = padded[:, global_index[3]]
            updated = values - pos_x * (values - west_value) - neg_x * (east_value - values) - pos_y * (values - south_value) - neg_y * (north_value - values)
            values = jnp.where(repeat < counts[:, None], updated, values)
        return values

    def propagate(spectra):
        shaped = spectra.reshape(NF, ND, PTS)
        moved = lax.map(per_frequency, (shaped, wave_speed, substeps.reshape(NF, ND)))
        return moved.reshape(NF * ND, PTS)

    def source_term(spectra):
        spectra_grid = spectra.reshape(NF, ND, PTS)
        rounded = spectra_grid.astype(jnp.bfloat16)

        def accumulate(total, index):
            matrix = blocks[index].astype(jnp.float32)
            first_freq = quad_index[0, index]
            second_freq = quad_index[1, index]
            third_freq = quad_index[2, index]
            target = quad_index[3, index]
            left_term = jnp.dot(matrix, rounded[first_freq].astype(jnp.float32), precision=lax.Precision.HIGHEST)
            right_term = jnp.dot(matrix.T, rounded[second_freq].astype(jnp.float32), precision=lax.Precision.HIGHEST)
            product = (left_term * right_term * spectra_grid[third_freq]).astype(jnp.bfloat16)
            part_term = jnp.dot(matrix, product.astype(jnp.float32), precision=lax.Precision.HIGHEST)
            return total.at[target].add(strength[index] * part_term), None

        total, unused = lax.scan(accumulate, jnp.zeros((NF, ND, PTS), jnp.float32), jnp.arange(NBLK, dtype=jnp.int32))
        return (spectra_grid + source_step * total).reshape(NF * ND, PTS)

    spectra = spectrum
    for repeat in range(STEPS):
        spectra = source_term(propagate(spectra))
    return spectra
```

```python
import functools
import math

import jax
import jax.numpy as jnp
import numpy as np
from jax import lax
from jax.experimental import pallas as pl
from jax.experimental.pallas import tpu as pltpu
from jax.sharding import PartitionSpec as P

NF = 36
ND = 64
SUB = 4
HALO = 128
SKEW = 2

courant_scale = 0.4
courant_limit = 0.45
source_step = 0.1

MESH = pl.DeviceIdType.MESH


def chunk_rows(rows):
    for size in (64, 72, 48, 40, 32, 24, 16, 8):
        if rows % size == 0:
            return size
    return rows


def sync(peers, spaces):
    me = lax.axis_index("comp")
    here = lax.axis_index("space")
    barrier = pltpu.get_barrier_semaphore()
    count = 0
    for k in range(1, peers):
        pl.semaphore_signal(
            barrier, inc=1, device_id={"comp": lax.rem(me + k, peers)}, device_id_type=MESH
        )
        count += 1
    if spaces:
        for k in (1, spaces - 1):
            pl.semaphore_signal(
                barrier, inc=1, device_id={"space": lax.rem(here + k, spaces)}, device_id_type=MESH
            )
            count += 1
    pl.semaphore_wait(barrier, count)


def propagate_kernel(
    peers,
    spaces,
    chunk,
    field_ref,
    columns_ref,
    current_ref,
    position_ref,
    points_ref,
    states,
    speed_x,
    speed_y,
    load_sem,
    halo_send,
    halo_recv,
    piece_send,
    piece_recv,
    own_sem,
):
    me = lax.axis_index("comp")
    here = lax.axis_index("space")
    rows = columns_ref.shape[0]
    tiles = position_ref.shape[0]
    chunks = rows // chunk
    has_left = here > 0
    has_right = here < spaces - 1

    loads = [
        pltpu.make_async_copy(
            field_ref.at[:, pl.ds(j * HALO, HALO)], states.at[0, j + 1], load_sem.at[j]
        )
        for j in range(tiles)
    ]
    for load in loads:
        load.start()

    @pl.when(jnp.logical_not(has_left))
    def _():
        for s in range(SUB):
            states[s, 0] = jnp.zeros((rows, HALO), jnp.float32)

    @pl.when(jnp.logical_not(has_right))
    def _():
        for s in range(SUB):
            states[s, tiles + 1] = jnp.zeros((rows, HALO), jnp.float32)

    sync(peers, spaces)

    def halo_copies(s, first, count):
        part = pl.ds(first, count)
        chunk_id = first // chunk
        to_left = pltpu.make_async_remote_copy(
            src_ref=states.at[s, 1, part],
            dst_ref=states.at[s, tiles + 1, part],
            send_sem=halo_send.at[s, 0],
            recv_sem=halo_recv.at[s, 0, chunk_id],
            device_id={"space": jnp.maximum(here - 1, 0)},
            device_id_type=MESH,
        )
        to_right = pltpu.make_async_remote_copy(
            src_ref=states.at[s, tiles, part],
            dst_ref=states.at[s, 0, part],
            send_sem=halo_send.at[s, 1],
            recv_sem=halo_recv.at[s, 1, chunk_id],
            device_id={"space": jnp.minimum(here + 1, spaces - 1)},
            device_id_type=MESH,
        )
        return to_left, to_right

    def send_halo(s, c):
        to_left, to_right = halo_copies(s, c * chunk, chunk)

        @pl.when(has_left)
        def _():
            to_left.start()

        @pl.when(has_right)
        def _():
            to_right.start()

    def wait_halo(s, c):
        to_left, to_right = halo_copies(s, c * chunk, chunk)

        @pl.when(has_right)
        def _():
            to_left.wait_recv()

        @pl.when(has_left)
        def _():
            to_right.wait_recv()

    def piece(k, first, count):
        target = lax.rem(me + k, peers)
        return pltpu.make_async_remote_copy(
            src_ref=states.at[SUB, target + 1, pl.ds(first, count)],
            dst_ref=points_ref.at[pl.ds(pl.multiple_of(me * rows + first, 8), count)],
            send_sem=piece_send.at[k],
            recv_sem=piece_recv.at[k],
            device_id={"comp": target},
            device_id_type=MESH,
        )

    order = sorted(range(1, peers), key=lambda k: abs(k - peers / 2))

    def send_pieces(c):
        for k in order:
            piece(k, c * chunk, chunk).start()

    def prepare(c):
        def per_tile(j, carry):
            east = jnp.broadcast_to(current_ref[j, 0:1, :], (8, HALO))
            north = jnp.broadcast_to(current_ref[j, 1:2, :], (8, HALO))

            def per_group(g, inner):
                at = pl.ds(pl.multiple_of(c * chunk + g * 8, 8), 8)
                values = columns_ref[at, :]
                scale = values[:, 2:3]
                along_x = (values[:, 0:1] + east) * scale
                along_y = (values[:, 1:2] + north) * scale
                speed_x[j, at] = jnp.clip(along_x, -courant_limit, courant_limit)
                speed_y[j, at] = jnp.clip(along_y, -courant_limit, courant_limit)
                return inner

            return lax.fori_loop(0, chunk // 8, per_group, carry, unroll=True)

        lax.fori_loop(0, tiles, per_tile, 0)

    def advance(s, c):
        def per_tile(j, carry):
            west, east, south, north = [
                jnp.broadcast_to(position_ref[j, d : d + 1, :], (8, HALO)) for d in range(4)
            ]

            def upwind(speed, near, far, before, here_tile, after):
                spot = jnp.where(speed > 0.0, near, far)
                lane = spot & (HALO - 1)
                taken = [
                    jnp.take_along_axis(tile, lane, axis=1, mode="promise_in_bounds")
                    for tile in (before, here_tile, after)
                ]
                value = jnp.where(
                    spot < HALO, taken[0], jnp.where(spot < 2 * HALO, taken[1], taken[2])
                )
                return jnp.abs(speed) * (here_tile - value)

            def per_group(g, inner):
                at = pl.ds(pl.multiple_of(c * chunk + g * 8, 8), 8)
                before = states[s, j, at]
                value = states[s, j + 1, at]
                after = states[s, j + 2, at]
                change = upwind(speed_x[j, at], west, east, before, value, after)
                change = change + upwind(speed_y[j, at], south, north, before, value, after)
                live = columns_ref[at, :][:, 3:4] > float(s)
                states[s + 1, j + 1, at] = jnp.where(live, value - change, value)
                return inner

            return lax.fori_loop(0, chunk // 8, per_group, carry, unroll=True)

        lax.fori_loop(0, tiles, per_tile, 0)

    for load in loads:
        load.wait()
    for c in range(chunks):
        send_halo(0, c)
    for wave in range(chunks + SKEW * (SUB - 1)):
        for s in reversed(range(SUB)):
            c = wave - SKEW * s
            if not 0 <= c < chunks:
                continue
            if s == 0:
                prepare(c)
            wait_halo(s, c)
            advance(s, c)
            if s + 1 < SUB:
                send_halo(s + 1, c)
            else:
                send_pieces(c)
    own = pltpu.make_async_copy(
        states.at[SUB, me + 1],
        points_ref.at[pl.ds(pl.multiple_of(me * rows, 8), rows)],
        own_sem,
    )
    own.start()
    own.wait()
    for s in range(SUB):
        to_left, to_right = halo_copies(s, 0, rows)

        @pl.when(has_left)
        def _():
            to_left.wait_send()

        @pl.when(has_right)
        def _():
            to_right.wait_send()

    for k in range(1, peers):
        whole = piece(k, 0, rows)
        whole.wait_send()
        whole.wait_recv()


def propagate(field, columns, current, position, peers, spaces):
    rows = field.shape[0]
    tiles = position.shape[0]
    chunk = chunk_rows(rows)
    vmem = pl.BlockSpec(memory_space=pltpu.VMEM)
    return pl.pallas_call(
        functools.partial(propagate_kernel, peers, spaces, chunk),
        out_shape=jax.ShapeDtypeStruct((peers * rows, HALO), jnp.float32),
        in_specs=[pl.BlockSpec(memory_space=pl.ANY), vmem, vmem, vmem],
        out_specs=vmem,
        scratch_shapes=[
            pltpu.VMEM((SUB + 1, tiles + 2, rows, HALO), jnp.float32),
            pltpu.VMEM((tiles, rows, HALO), jnp.float32),
            pltpu.VMEM((tiles, rows, HALO), jnp.float32),
            pltpu.SemaphoreType.DMA((tiles,)),
            pltpu.SemaphoreType.DMA((SUB, 2)),
            pltpu.SemaphoreType.DMA((SUB, 2, rows // chunk)),
            pltpu.SemaphoreType.DMA((peers,)),
            pltpu.SemaphoreType.DMA((peers,)),
            pltpu.SemaphoreType.DMA,
        ],
        compiler_params=pltpu.CompilerParams(collective_id=0, has_side_effects=True),
    )(field, columns, current, position)


def source_kernel(batch, quad_ref, strength_ref, points_ref, blocks_ref, out_ref, rounded):
    total = blocks_ref.shape[0]

    def fill(f, carry):
        value = points_ref[f]
        rounded[f] = value.astype(jnp.bfloat16)
        out_ref[f] = value
        return carry

    lax.fori_loop(0, NF, fill, 0, unroll=4)

    def step(i, carry):
        parts = []
        for b in range(batch):
            j = i * batch + b
            block = blocks_ref[j]
            left = jnp.dot(block, rounded[quad_ref[0, j]], preferred_element_type=jnp.float32)
            right = lax.dot_general(
                block,
                rounded[quad_ref[1, j]],
                (((0,), (0,)), ((), ())),
                preferred_element_type=jnp.float32,
            )
            product = (left * right * points_ref[quad_ref[2, j]]).astype(jnp.bfloat16)
            part = jnp.dot(block, product, preferred_element_type=jnp.float32)
            parts.append(part * (strength_ref[j] * source_step))
        for b in range(batch):
            target = quad_ref[3, i * batch + b]
            out_ref[target] = out_ref[target] + parts[b]
        return carry

    lax.fori_loop(0, total // batch, step, 0)


def source_term(points, blocks, quad_index, strength):
    width = points.shape[1]
    vmem = pl.BlockSpec(memory_space=pltpu.VMEM)
    smem = pl.BlockSpec(memory_space=pltpu.SMEM)
    out = pl.pallas_call(
        functools.partial(source_kernel, math.gcd(blocks.shape[0], 4)),
        out_shape=jax.ShapeDtypeStruct((NF, ND, width), jnp.float32),
        in_specs=[smem, smem, vmem, vmem],
        out_specs=vmem,
        scratch_shapes=[pltpu.VMEM((NF, ND, width), jnp.bfloat16)],
    )(quad_index, strength, points.reshape(NF, ND, width), blocks)
    return out.reshape(NF * ND, width)


def home_kernel(peers, points_ref, out_ref, send_sem, recv_sem, own_sem):
    me = lax.axis_index("comp")
    rows = out_ref.shape[0]
    place = pl.ds(pl.multiple_of(me * HALO, HALO), HALO)
    own = pltpu.make_async_copy(
        points_ref.at[pl.ds(pl.multiple_of(me * rows, 8), rows)], out_ref.at[:, place], own_sem
    )
    own.start()
    sync(peers, 0)
    copies = []
    for k in sorted(range(1, peers), key=lambda k: abs(k - peers / 2)):
        target = lax.rem(me + k, peers)
        copy = pltpu.make_async_remote_copy(
            src_ref=points_ref.at[pl.ds(pl.multiple_of(target * rows, 8), rows)],
            dst_ref=out_ref.at[:, place],
            send_sem=send_sem.at[k],
            recv_sem=recv_sem.at[k],
            device_id={"comp": target},
            device_id_type=MESH,
        )
        copy.start()
        copies.append(copy)
    own.wait()
    for copy in copies:
        copy.wait()


def send_home(points, peers):
    rows = points.shape[0] // peers
    return pl.pallas_call(
        functools.partial(home_kernel, peers),
        out_shape=jax.ShapeDtypeStruct((rows, peers * HALO), jnp.float32),
        in_specs=[pl.BlockSpec(memory_space=pltpu.VMEM)],
        out_specs=pl.BlockSpec(memory_space=pltpu.VMEM),
        scratch_shapes=[
            pltpu.SemaphoreType.DMA((peers,)),
            pltpu.SemaphoreType.DMA((peers,)),
            pltpu.SemaphoreType.DMA,
        ],
        compiler_params=pltpu.CompilerParams(collective_id=1, has_side_effects=True),
    )(points)


def shards(
    spectrum,
    wave_speed,
    current_east,
    current_north,
    substeps,
    neighbours,
    blocks,
    quad_index,
    strength,
):
    peers = lax.axis_size("comp")
    spaces = lax.axis_size("space")
    rows, width = spectrum.shape
    assert width == peers * HALO
    first = lax.axis_index("comp") * rows
    angles = (np.arange(ND, dtype=np.float32) + np.float32(0.5)) * np.float32(2.0 * math.pi / ND)
    counts = substeps.astype(jnp.float32)
    columns = jnp.stack(
        [
            (wave_speed[:, None] * np.cos(angles)[None, :]).reshape(NF * ND),
            (wave_speed[:, None] * np.sin(angles)[None, :]).reshape(NF * ND),
            courant_scale / counts,
            counts,
        ],
        axis=1,
    )
    columns = lax.dynamic_slice_in_dim(columns, first, rows)
    tiles = width // HALO
    current = jnp.stack(
        [current_east.reshape(tiles, HALO), current_north.reshape(tiles, HALO)], axis=1
    )
    position = neighbours.reshape(4, tiles, HALO) - HALO * jnp.arange(tiles)[None, :, None]
    position = position.transpose(1, 0, 2)
    points = propagate(spectrum, columns, current, position, peers, spaces)
    points = source_term(points, blocks, quad_index, strength)
    return send_home(points, peers)


def solution(mesh):
    in_specs = (
        P("comp", ("grp", "space")),
        P(),
        P(("grp", "space")),
        P(("grp", "space")),
        P(),
        P(None, ("grp", "space")),
        P(),
        P(),
        P(),
    )
    out_specs = P("comp", ("grp", "space"))
    return jax.shard_map(shards, mesh=mesh, in_specs=in_specs, out_specs=out_specs, check_vma=False)
```

```python
import functools
import math

import jax
import jax.numpy as jnp
import numpy as np
from jax import lax
from jax.experimental import pallas as pl
from jax.experimental.pallas import tpu as pltpu
from jax.sharding import PartitionSpec as P

NF = 36
ND = 64
SUB = 4
HALO = 128
SKEW = 1

courant_scale = 0.4
courant_limit = 0.45
source_step = 0.1

MESH = pl.DeviceIdType.MESH


def chunk_rows(rows):
    for size in (64, 72, 48, 40, 32, 24, 16, 8):
        if rows % size == 0:
            return size
    return rows


def sync(peers, spaces):
    me = lax.axis_index("comp")
    here = lax.axis_index("space")
    barrier = pltpu.get_barrier_semaphore()
    count = 0
    for k in range(1, peers):
        pl.semaphore_signal(
            barrier, inc=1, device_id={"comp": lax.rem(me + k, peers)}, device_id_type=MESH
        )
        count += 1
    if spaces:
        for k in (1, spaces - 1):
            pl.semaphore_signal(
                barrier, inc=1, device_id={"space": lax.rem(here + k, spaces)}, device_id_type=MESH
            )
            count += 1
    pl.semaphore_wait(barrier, count)


def propagate_kernel(
    peers,
    spaces,
    chunk,
    field_ref,
    wave_ref,
    substeps_ref,
    trig_ref,
    east_ref,
    north_ref,
    neighbour_ref,
    points_ref,
    states,
    speed_x,
    speed_y,
    repeats,
    load_sem,
    halo_send,
    halo_recv,
    piece_send,
    piece_recv,
    own_sem,
):
    me = lax.axis_index("comp")
    here = lax.axis_index("space")
    rows, width = field_ref.shape
    tiles = width // HALO
    chunks = rows // chunk
    has_left = here > 0
    has_right = here < spaces - 1

    loads = [
        pltpu.make_async_copy(
            field_ref.at[:, pl.ds(j * HALO, HALO)], states.at[0, j + 1], load_sem.at[j]
        )
        for j in range(tiles)
    ]
    for load in loads:
        load.start()

    @pl.when(jnp.logical_not(has_left))
    def _():
        for s in range(SUB):
            states[s, 0] = jnp.zeros((rows, HALO), jnp.float32)

    @pl.when(jnp.logical_not(has_right))
    def _():
        for s in range(SUB):
            states[s, tiles + 1] = jnp.zeros((rows, HALO), jnp.float32)

    sync(peers, spaces)

    def halo_copies(s, first, count):
        part = pl.ds(first, count)
        chunk_id = first // chunk
        to_left = pltpu.make_async_remote_copy(
            src_ref=states.at[s, 1, part],
            dst_ref=states.at[s, tiles + 1, part],
            send_sem=halo_send.at[s, 0],
            recv_sem=halo_recv.at[s, 0, chunk_id],
            device_id={"space": jnp.maximum(here - 1, 0)},
            device_id_type=MESH,
        )
        to_right = pltpu.make_async_remote_copy(
            src_ref=states.at[s, tiles, part],
            dst_ref=states.at[s, 0, part],
            send_sem=halo_send.at[s, 1],
            recv_sem=halo_recv.at[s, 1, chunk_id],
            device_id={"space": jnp.minimum(here + 1, spaces - 1)},
            device_id_type=MESH,
        )
        return to_left, to_right

    def send_halo(s, c):
        to_left, to_right = halo_copies(s, c * chunk, chunk)

        @pl.when(has_left)
        def _():
            to_left.start()

        @pl.when(has_right)
        def _():
            to_right.start()

    def wait_halo(s, c):
        to_left, to_right = halo_copies(s, c * chunk, chunk)

        @pl.when(has_right)
        def _():
            to_left.wait_recv()

        @pl.when(has_left)
        def _():
            to_right.wait_recv()

    def piece(k, first, count):
        target = lax.rem(me + k, peers)
        return pltpu.make_async_remote_copy(
            src_ref=states.at[SUB, target + 1, pl.ds(first, count)],
            dst_ref=points_ref.at[pl.ds(pl.multiple_of(me * rows + first, 8), count)],
            send_sem=piece_send.at[k],
            recv_sem=piece_recv.at[k],
            device_id={"comp": target},
            device_id_type=MESH,
        )

    order = sorted(range(1, peers), key=lambda k: abs(k - peers / 2))

    def send_pieces(c):
        for k in order:
            piece(k, c * chunk, chunk).start()

    def lanes(j):
        return pl.ds(pl.multiple_of(j * HALO, HALO), HALO)

    sublane = lax.broadcasted_iota(jnp.int32, (8, HALO), 0)

    def prepare(c):
        def per_group(g, carry):
            row = pl.multiple_of(c * chunk + g * 8, 8)
            at = pl.ds(row, 8)
            component = me * rows + row
            speed = wave_ref[component // ND]
            turn = pl.ds(pl.multiple_of(lax.rem(component, ND), 8), 8)
            own_x = trig_ref[0, turn, :] * speed
            own_y = trig_ref[1, turn, :] * speed
            taken = jnp.full((8, HALO), substeps_ref[component], jnp.int32)
            for i in range(1, 8):
                taken = jnp.where(sublane == i, substeps_ref[component + i], taken)
            count = taken.astype(jnp.float32)
            repeats[at] = count
            scale = courant_scale / count

            def per_tile(j, inner):
                along_x = (own_x + east_ref[0:1, lanes(j)]) * scale
                along_y = (own_y + north_ref[0:1, lanes(j)]) * scale
                speed_x[j, at] = jnp.clip(along_x, -courant_limit, courant_limit)
                speed_y[j, at] = jnp.clip(along_y, -courant_limit, courant_limit)
                return inner

            return lax.fori_loop(0, tiles, per_tile, carry, unroll=tiles <= 4)

        lax.fori_loop(0, chunk // 8, per_group, 0)

    def advance(s, c):
        def per_tile(j, carry):
            west, east, south, north = [
                jnp.broadcast_to(neighbour_ref[d : d + 1, lanes(j)] - j * HALO, (8, HALO))
                for d in range(4)
            ]

            def upwind(speed, near, far, before, here_tile, after):
                spot = jnp.where(speed > 0.0, near, far)
                lane = spot & (HALO - 1)
                taken = [
                    jnp.take_along_axis(tile, lane, axis=1, mode="promise_in_bounds")
                    for tile in (before, here_tile, after)
                ]
                value = jnp.where(
                    spot < HALO, taken[0], jnp.where(spot < 2 * HALO, taken[1], taken[2])
                )
                return jnp.abs(speed) * (here_tile - value)

            def per_group(g, inner):
                at = pl.ds(pl.multiple_of(c * chunk + g * 8, 8), 8)
                before = states[s, j, at]
                value = states[s, j + 1, at]
                after = states[s, j + 2, at]
                change = upwind(speed_x[j, at], west, east, before, value, after)
                change = change + upwind(speed_y[j, at], south, north, before, value, after)
                if s > 0:
                    change = jnp.where(repeats[at] > float(s), change, 0.0)
                states[s + 1, j + 1, at] = value - change
                return inner

            return lax.fori_loop(0, chunk // 8, per_group, carry, unroll=True)

        lax.fori_loop(0, tiles, per_tile, 0)

    for load in loads:
        load.wait()
    for c in range(chunks):
        send_halo(0, c)
    for wave in range(chunks + SKEW * (SUB - 1)):
        for s in reversed(range(SUB)):
            c = wave - SKEW * s
            if not 0 <= c < chunks:
                continue
            if s == 0:
                prepare(c)
            wait_halo(s, c)
            advance(s, c)
            if s + 1 < SUB:
                send_halo(s + 1, c)
            else:
                send_pieces(c)
    own = pltpu.make_async_copy(
        states.at[SUB, me + 1],
        points_ref.at[pl.ds(pl.multiple_of(me * rows, 8), rows)],
        own_sem,
    )
    own.start()
    own.wait()
    for s in range(SUB):
        to_left, to_right = halo_copies(s, 0, rows)

        @pl.when(has_left)
        def _():
            to_left.wait_send()

        @pl.when(has_right)
        def _():
            to_right.wait_send()

    for k in range(1, peers):
        whole = piece(k, 0, rows)
        whole.wait_send()
        whole.wait_recv()


def propagate(field, wave_speed, substeps, east, north, neighbours, peers, spaces):
    rows, width = field.shape
    tiles = width // HALO
    chunk = chunk_rows(rows)
    angles = (np.arange(ND, dtype=np.float32) + np.float32(0.5)) * np.float32(2.0 * math.pi / ND)
    trig = np.stack([np.cos(angles), np.sin(angles)])
    trig = np.ascontiguousarray(np.broadcast_to(trig[:, :, None], (2, ND, HALO)))
    vmem = pl.BlockSpec(memory_space=pltpu.VMEM)
    smem = pl.BlockSpec(memory_space=pltpu.SMEM)
    return pl.pallas_call(
        functools.partial(propagate_kernel, peers, spaces, chunk),
        out_shape=jax.ShapeDtypeStruct((peers * rows, HALO), jnp.float32),
        in_specs=[pl.BlockSpec(memory_space=pl.ANY), smem, smem, vmem, vmem, vmem, vmem],
        out_specs=vmem,
        scratch_shapes=[
            pltpu.VMEM((SUB + 1, tiles + 2, rows, HALO), jnp.float32),
            pltpu.VMEM((tiles, rows, HALO), jnp.float32),
            pltpu.VMEM((tiles, rows, HALO), jnp.float32),
            pltpu.VMEM((rows, HALO), jnp.float32),
            pltpu.SemaphoreType.DMA((tiles,)),
            pltpu.SemaphoreType.DMA((SUB, 2)),
            pltpu.SemaphoreType.DMA((SUB, 2, rows // chunk)),
            pltpu.SemaphoreType.DMA((peers,)),
            pltpu.SemaphoreType.DMA((peers,)),
            pltpu.SemaphoreType.DMA,
        ],
        compiler_params=pltpu.CompilerParams(collective_id=0, has_side_effects=True),
    )(
        field,
        wave_speed,
        substeps,
        jnp.asarray(trig),
        east.reshape(1, width),
        north.reshape(1, width),
        neighbours,
    )


def source_kernel(batch, quad_ref, strength_ref, points_ref, blocks_ref, out_ref, rounded):
    total = blocks_ref.shape[0]

    def fill(f, carry):
        value = points_ref[f]
        rounded[f] = value.astype(jnp.bfloat16)
        out_ref[f] = value
        return carry

    lax.fori_loop(0, NF, fill, 0, unroll=4)

    def step(i, carry):
        parts = []
        for b in range(batch):
            j = i * batch + b
            block = blocks_ref[j]
            left = jnp.dot(block, rounded[quad_ref[0, j]], preferred_element_type=jnp.float32)
            right = lax.dot_general(
                block,
                rounded[quad_ref[1, j]],
                (((0,), (0,)), ((), ())),
                preferred_element_type=jnp.float32,
            )
            product = (left * right * points_ref[quad_ref[2, j]]).astype(jnp.bfloat16)
            part = jnp.dot(block, product, preferred_element_type=jnp.float32)
            parts.append(part * (strength_ref[j] * source_step))
        for b in range(batch):
            target = quad_ref[3, i * batch + b]
            out_ref[target] = out_ref[target] + parts[b]
        return carry

    lax.fori_loop(0, total // batch, step, 0)


def source_term(points, blocks, quad_index, strength):
    width = points.shape[1]
    vmem = pl.BlockSpec(memory_space=pltpu.VMEM)
    smem = pl.BlockSpec(memory_space=pltpu.SMEM)
    out = pl.pallas_call(
        functools.partial(source_kernel, math.gcd(blocks.shape[0], 16)),
        out_shape=jax.ShapeDtypeStruct((NF, ND, width), jnp.float32),
        in_specs=[smem, smem, vmem, vmem],
        out_specs=vmem,
        scratch_shapes=[pltpu.VMEM((NF, ND, width), jnp.bfloat16)],
    )(quad_index, strength, points.reshape(NF, ND, width), blocks)
    return out.reshape(NF * ND, width)


def home_kernel(peers, points_ref, out_ref, send_sem, recv_sem, own_sem):
    me = lax.axis_index("comp")
    rows = out_ref.shape[0]
    place = pl.ds(pl.multiple_of(me * HALO, HALO), HALO)
    own = pltpu.make_async_copy(
        points_ref.at[pl.ds(pl.multiple_of(me * rows, 8), rows)], out_ref.at[:, place], own_sem
    )
    own.start()
    sync(peers, 0)
    copies = []
    for k in sorted(range(1, peers), key=lambda k: abs(k - peers / 2)):
        target = lax.rem(me + k, peers)
        copy = pltpu.make_async_remote_copy(
            src_ref=points_ref.at[pl.ds(pl.multiple_of(target * rows, 8), rows)],
            dst_ref=out_ref.at[:, place],
            send_sem=send_sem.at[k],
            recv_sem=recv_sem.at[k],
            device_id={"comp": target},
            device_id_type=MESH,
        )
        copy.start()
        copies.append(copy)
    own.wait()
    for copy in copies:
        copy.wait()


def send_home(points, peers):
    rows = points.shape[0] // peers
    return pl.pallas_call(
        functools.partial(home_kernel, peers),
        out_shape=jax.ShapeDtypeStruct((rows, peers * HALO), jnp.float32),
        in_specs=[pl.BlockSpec(memory_space=pltpu.VMEM)],
        out_specs=pl.BlockSpec(memory_space=pltpu.VMEM),
        scratch_shapes=[
            pltpu.SemaphoreType.DMA((peers,)),
            pltpu.SemaphoreType.DMA((peers,)),
            pltpu.SemaphoreType.DMA,
        ],
        compiler_params=pltpu.CompilerParams(collective_id=1, has_side_effects=True),
    )(points)


def shards(
    spectrum,
    wave_speed,
    current_east,
    current_north,
    substeps,
    neighbours,
    blocks,
    quad_index,
    strength,
):
    peers = lax.axis_size("comp")
    spaces = lax.axis_size("space")
    rows, width = spectrum.shape
    assert width == peers * HALO
    points = propagate(
        spectrum, wave_speed, substeps, current_east, current_north, neighbours, peers, spaces
    )
    points = source_term(points, blocks, quad_index, strength)
    return send_home(points, peers)


def solution(mesh):
    in_specs = (
        P("comp", ("grp", "space")),
        P(),
        P(("grp", "space")),
        P(("grp", "space")),
        P(),
        P(None, ("grp", "space")),
        P(),
        P(),
        P(),
    )
    out_specs = P("comp", ("grp", "space"))
    return jax.shard_map(shards, mesh=mesh, in_specs=in_specs, out_specs=out_specs, check_vma=False)
```

```python
import functools
import math

import jax
import jax.numpy as jnp
import numpy as np
from jax import lax
from jax.experimental import pallas as pl
from jax.experimental.pallas import tpu as pltpu
from jax.sharding import PartitionSpec as P

NF = 36
ND = 64
SUB = 4
HALO = 128
SKEW = 2

courant_scale = 0.4
courant_limit = 0.45
source_step = 0.1

MESH = pl.DeviceIdType.MESH


def chunk_rows(rows):
    for size in (64, 72, 48, 40, 32, 24, 16, 8):
        if rows % size == 0:
            return size
    return rows


def sync(peers, spaces):
    me = lax.axis_index("comp")
    here = lax.axis_index("space")
    barrier = pltpu.get_barrier_semaphore()
    count = 0
    for k in range(1, peers):
        pl.semaphore_signal(
            barrier, inc=1, device_id={"comp": lax.rem(me + k, peers)}, device_id_type=MESH
        )
        count += 1
    if spaces:
        for k in (1, spaces - 1):
            pl.semaphore_signal(
                barrier, inc=1, device_id={"space": lax.rem(here + k, spaces)}, device_id_type=MESH
            )
            count += 1
    pl.semaphore_wait(barrier, count)


def propagate_kernel(
    peers,
    spaces,
    chunk,
    field_ref,
    wave_ref,
    substeps_ref,
    trig_ref,
    east_ref,
    north_ref,
    neighbour_ref,
    points_ref,
    states,
    speed_x,
    speed_y,
    repeats,
    selector,
    load_sem,
    halo_send,
    halo_recv,
    piece_send,
    piece_recv,
    own_sem,
):
    me = lax.axis_index("comp")
    here = lax.axis_index("space")
    rows, width = field_ref.shape
    tiles = width // HALO
    chunks = rows // chunk
    has_left = here > 0
    has_right = here < spaces - 1

    loads = [
        pltpu.make_async_copy(
            field_ref.at[:, pl.ds(j * HALO, HALO)], states.at[0, j + 1], load_sem.at[j]
        )
        for j in range(tiles)
    ]
    for load in loads:
        load.start()

    @pl.when(jnp.logical_not(has_left))
    def _():
        for s in range(SUB):
            states[s, 0] = jnp.zeros((rows, HALO), jnp.float32)

    @pl.when(jnp.logical_not(has_right))
    def _():
        for s in range(SUB):
            states[s, tiles + 1] = jnp.zeros((rows, HALO), jnp.float32)

    sync(peers, spaces)

    def halo_copies(s, first, count):
        part = pl.ds(first, count)
        chunk_id = first // chunk
        to_left = pltpu.make_async_remote_copy(
            src_ref=states.at[s, 1, part],
            dst_ref=states.at[s, tiles + 1, part],
            send_sem=halo_send.at[s, 0],
            recv_sem=halo_recv.at[s, 0, chunk_id],
            device_id={"space": jnp.maximum(here - 1, 0)},
            device_id_type=MESH,
        )
        to_right = pltpu.make_async_remote_copy(
            src_ref=states.at[s, tiles, part],
            dst_ref=states.at[s, 0, part],
            send_sem=halo_send.at[s, 1],
            recv_sem=halo_recv.at[s, 1, chunk_id],
            device_id={"space": jnp.minimum(here + 1, spaces - 1)},
            device_id_type=MESH,
        )
        return to_left, to_right

    def send_halo(s, c):
        to_left, to_right = halo_copies(s, c * chunk, chunk)

        @pl.when(has_left)
        def _():
            to_left.start()

        @pl.when(has_right)
        def _():
            to_right.start()

    def wait_halo(s, c):
        to_left, to_right = halo_copies(s, c * chunk, chunk)

        @pl.when(has_right)
        def _():
            to_left.wait_recv()

        @pl.when(has_left)
        def _():
            to_right.wait_recv()

    def piece(k, first, count):
        target = lax.rem(me + k, peers)
        return pltpu.make_async_remote_copy(
            src_ref=states.at[SUB, target + 1, pl.ds(first, count)],
            dst_ref=points_ref.at[pl.ds(pl.multiple_of(me * rows + first, 8), count)],
            send_sem=piece_send.at[k],
            recv_sem=piece_recv.at[k],
            device_id={"comp": target},
            device_id_type=MESH,
        )

    order = sorted(range(1, peers), key=lambda k: abs(k - peers / 2))

    def send_pieces(c):
        for k in order:
            piece(k, c * chunk, chunk).start()

    def lanes(j):
        return pl.ds(pl.multiple_of(j * HALO, HALO), HALO)

    sublane = lax.broadcasted_iota(jnp.int32, (8, HALO), 0)

    def prepare(c):
        def per_group(g, carry):
            row = pl.multiple_of(c * chunk + g * 8, 8)
            at = pl.ds(row, 8)
            component = me * rows + row
            speed = wave_ref[component // ND]
            turn = pl.ds(pl.multiple_of(lax.rem(component, ND), 8), 8)
            own_x = trig_ref[0, turn, :] * speed
            own_y = trig_ref[1, turn, :] * speed
            taken = jnp.full((8, HALO), substeps_ref[component], jnp.int32)
            for i in range(1, 8):
                taken = jnp.where(sublane == i, substeps_ref[component + i], taken)
            count = taken.astype(jnp.float32)
            repeats[at] = count
            scale = courant_scale / count

            def per_tile(j, inner):
                along_x = (own_x + east_ref[0:1, lanes(j)]) * scale
                along_y = (own_y + north_ref[0:1, lanes(j)]) * scale
                speed_x[j, at] = jnp.clip(along_x, -courant_limit, courant_limit)
                speed_y[j, at] = jnp.clip(along_y, -courant_limit, courant_limit)
                return inner

            return lax.fori_loop(0, tiles, per_tile, carry, unroll=tiles <= 4)

        lax.fori_loop(0, chunk // 8, per_group, 0)

    def choices(j, carry):
        spot = lax.broadcasted_iota(jnp.int32, (2 * HALO, HALO), 0)
        for d in range(4):
            wanted = neighbour_ref[d : d + 1, lanes(j)] - (j + d % 2) * HALO
            chosen = jnp.where(spot == wanted, 1.0, 0.0).astype(jnp.bfloat16)
            half = d // 2 * HALO
            selector[j, d % 2, :, half : half + HALO] = chosen
        return carry

    def split(x):
        high = x.astype(jnp.bfloat16)
        rest = x - high.astype(jnp.float32)
        middle = rest.astype(jnp.bfloat16)
        low = (rest - middle.astype(jnp.float32)).astype(jnp.bfloat16)
        return high, middle, low

    def pick(first, second, chosen):
        pairs = [jnp.concatenate(pair, axis=1) for pair in zip(first, second)]
        if chunk % 16 == 0:
            taken = jnp.dot(
                jnp.concatenate(pairs, axis=0), chosen, preferred_element_type=jnp.float32
            )
            terms = [taken[i * chunk : (i + 1) * chunk] for i in range(3)]
        else:
            terms = [jnp.dot(p, chosen, preferred_element_type=jnp.float32) for p in pairs]
        taken = terms[0] + terms[1] + terms[2]
        return taken[:, :HALO], taken[:, HALO:]

    def advance(s, c):
        at = pl.ds(c * chunk, chunk)

        def per_tile(j, carry):
            value = states[s, j + 1, at]
            here_split = split(value)
            west, south = pick(split(states[s, j, at]), here_split, selector[j, 0])
            east, north = pick(here_split, split(states[s, j + 2, at]), selector[j, 1])
            along_x = speed_x[j, at]
            along_y = speed_y[j, at]
            change = jnp.abs(along_x) * (value - jnp.where(along_x > 0.0, west, east))
            change = change + jnp.abs(along_y) * (value - jnp.where(along_y > 0.0, south, north))
            if s > 0:
                change = jnp.where(repeats[at] > float(s), change, 0.0)
            states[s + 1, j + 1, at] = value - change
            return carry

        lax.fori_loop(0, tiles, per_tile, 0, unroll=2)

    for load in loads:
        load.wait()
    for c in range(chunks):
        send_halo(0, c)
    lax.fori_loop(0, tiles, choices, 0)
    for wave in range(chunks + SKEW * (SUB - 1)):
        for s in reversed(range(SUB)):
            c = wave - SKEW * s
            if not 0 <= c < chunks:
                continue
            if s == 0:
                prepare(c)
            wait_halo(s, c)
            advance(s, c)
            if s + 1 < SUB:
                send_halo(s + 1, c)
            else:
                send_pieces(c)
    own = pltpu.make_async_copy(
        states.at[SUB, me + 1],
        points_ref.at[pl.ds(pl.multiple_of(me * rows, 8), rows)],
        own_sem,
    )
    own.start()
    own.wait()
    for s in range(SUB):
        to_left, to_right = halo_copies(s, 0, rows)

        @pl.when(has_left)
        def _():
            to_left.wait_send()

        @pl.when(has_right)
        def _():
            to_right.wait_send()

    for k in range(1, peers):
        whole = piece(k, 0, rows)
        whole.wait_send()
        whole.wait_recv()


def propagate(field, wave_speed, substeps, east, north, neighbours, peers, spaces):
    rows, width = field.shape
    tiles = width // HALO
    chunk = chunk_rows(rows)
    angles = (np.arange(ND, dtype=np.float32) + np.float32(0.5)) * np.float32(2.0 * math.pi / ND)
    trig = np.stack([np.cos(angles), np.sin(angles)])
    trig = np.ascontiguousarray(np.broadcast_to(trig[:, :, None], (2, ND, HALO)))
    vmem = pl.BlockSpec(memory_space=pltpu.VMEM)
    smem = pl.BlockSpec(memory_space=pltpu.SMEM)
    return pl.pallas_call(
        functools.partial(propagate_kernel, peers, spaces, chunk),
        out_shape=jax.ShapeDtypeStruct((peers * rows, HALO), jnp.float32),
        in_specs=[pl.BlockSpec(memory_space=pl.ANY), smem, smem, vmem, vmem, vmem, vmem],
        out_specs=vmem,
        scratch_shapes=[
            pltpu.VMEM((SUB + 1, tiles + 2, rows, HALO), jnp.float32),
            pltpu.VMEM((tiles, rows, HALO), jnp.float32),
            pltpu.VMEM((tiles, rows, HALO), jnp.float32),
            pltpu.VMEM((rows, HALO), jnp.float32),
            pltpu.VMEM((tiles, 2, 2 * HALO, 2 * HALO), jnp.bfloat16),
            pltpu.SemaphoreType.DMA((tiles,)),
            pltpu.SemaphoreType.DMA((SUB, 2)),
            pltpu.SemaphoreType.DMA((SUB, 2, rows // chunk)),
            pltpu.SemaphoreType.DMA((peers,)),
            pltpu.SemaphoreType.DMA((peers,)),
            pltpu.SemaphoreType.DMA,
        ],
        compiler_params=pltpu.CompilerParams(collective_id=0, has_side_effects=True),
    )(
        field,
        wave_speed,
        substeps,
        jnp.asarray(trig),
        east.reshape(1, width),
        north.reshape(1, width),
        neighbours,
    )


def source_kernel(batch, quad_ref, strength_ref, points_ref, blocks_ref, out_ref, rounded, products):
    total = blocks_ref.shape[0]

    def fill(f, carry):
        value = points_ref[f]
        rounded[f] = value.astype(jnp.bfloat16)
        out_ref[f] = value
        return carry

    lax.fori_loop(0, NF, fill, 0, unroll=4)

    def step(i, carry):
        for b in range(batch):
            j = i * batch + b
            block = blocks_ref[j]
            left = jnp.dot(block, rounded[quad_ref[0, j]], preferred_element_type=jnp.float32)
            right = lax.dot_general(
                block,
                rounded[quad_ref[1, j]],
                (((0,), (0,)), ((), ())),
                preferred_element_type=jnp.float32,
            )
            products[b] = (left * right * points_ref[quad_ref[2, j]]).astype(jnp.bfloat16)
        parts = []
        for b in range(batch):
            j = i * batch + b
            part = jnp.dot(blocks_ref[j], products[b], preferred_element_type=jnp.float32)
            parts.append(part * (strength_ref[j] * source_step))
        for b in range(batch):
            target = quad_ref[3, i * batch + b]
            out_ref[target] = out_ref[target] + parts[b]
        return carry

    lax.fori_loop(0, total // batch, step, 0)


def source_term(points, blocks, quad_index, strength):
    width = points.shape[1]
    vmem = pl.BlockSpec(memory_space=pltpu.VMEM)
    smem = pl.BlockSpec(memory_space=pltpu.SMEM)
    batch = math.gcd(blocks.shape[0], 16)
    out = pl.pallas_call(
        functools.partial(source_kernel, batch),
        out_shape=jax.ShapeDtypeStruct((NF, ND, width), jnp.float32),
        in_specs=[smem, smem, vmem, vmem],
        out_specs=vmem,
        scratch_shapes=[
            pltpu.VMEM((NF, ND, width), jnp.bfloat16),
            pltpu.VMEM((batch, ND, width), jnp.bfloat16),
        ],
    )(quad_index, strength, points.reshape(NF, ND, width), blocks)
    return out.reshape(NF * ND, width)


def home_kernel(peers, points_ref, out_ref, send_sem, recv_sem, own_sem):
    me = lax.axis_index("comp")
    rows = out_ref.shape[0]
    place = pl.ds(pl.multiple_of(me * HALO, HALO), HALO)
    own = pltpu.make_async_copy(
        points_ref.at[pl.ds(pl.multiple_of(me * rows, 8), rows)], out_ref.at[:, place], own_sem
    )
    own.start()
    sync(peers, 0)
    copies = []
    for k in sorted(range(1, peers), key=lambda k: abs(k - peers / 2)):
        target = lax.rem(me + k, peers)
        copy = pltpu.make_async_remote_copy(
            src_ref=points_ref.at[pl.ds(pl.multiple_of(target * rows, 8), rows)],
            dst_ref=out_ref.at[:, place],
            send_sem=send_sem.at[k],
            recv_sem=recv_sem.at[k],
            device_id={"comp": target},
            device_id_type=MESH,
        )
        copy.start()
        copies.append(copy)
    own.wait()
    for copy in copies:
        copy.wait()


def send_home(points, peers):
    rows = points.shape[0] // peers
    return pl.pallas_call(
        functools.partial(home_kernel, peers),
        out_shape=jax.ShapeDtypeStruct((rows, peers * HALO), jnp.float32),
        in_specs=[pl.BlockSpec(memory_space=pltpu.VMEM)],
        out_specs=pl.BlockSpec(memory_space=pltpu.VMEM),
        scratch_shapes=[
            pltpu.SemaphoreType.DMA((peers,)),
            pltpu.SemaphoreType.DMA((peers,)),
            pltpu.SemaphoreType.DMA,
        ],
        compiler_params=pltpu.CompilerParams(collective_id=1, has_side_effects=True),
    )(points)


def shards(
    spectrum,
    wave_speed,
    current_east,
    current_north,
    substeps,
    neighbours,
    blocks,
    quad_index,
    strength,
):
    peers = lax.axis_size("comp")
    spaces = lax.axis_size("space")
    rows, width = spectrum.shape
    assert width == peers * HALO
    points = propagate(
        spectrum, wave_speed, substeps, current_east, current_north, neighbours, peers, spaces
    )
    points = source_term(points, blocks, quad_index, strength)
    return send_home(points, peers)


def solution(mesh):
    in_specs = (
        P("comp", ("grp", "space")),
        P(),
        P(("grp", "space")),
        P(("grp", "space")),
        P(),
        P(None, ("grp", "space")),
        P(),
        P(),
        P(),
    )
    out_specs = P("comp", ("grp", "space"))
    return jax.shard_map(shards, mesh=mesh, in_specs=in_specs, out_specs=out_specs, check_vma=False)
```

```python
import functools
import math

import jax
import jax.numpy as jnp
import numpy as np
from jax import lax
from jax.experimental import pallas as pl
from jax.experimental.pallas import tpu as pltpu
from jax.sharding import PartitionSpec as P

NF = 36
ND = 64
SUB = 4
HALO = 128
SKEW = 2

courant_scale = 0.4
courant_limit = 0.45
source_step = 0.1

MESH = pl.DeviceIdType.MESH


def chunk_rows(rows):
    for size in (64, 72, 48, 40, 32, 24, 16, 8):
        if rows % size == 0:
            return size
    return rows


def sync(peers, spaces):
    me = lax.axis_index("comp")
    here = lax.axis_index("space")
    barrier = pltpu.get_barrier_semaphore()
    count = 0
    for k in range(1, peers):
        pl.semaphore_signal(
            barrier, inc=1, device_id={"comp": lax.rem(me + k, peers)}, device_id_type=MESH
        )
        count += 1
    if spaces:
        for k in (1, spaces - 1):
            pl.semaphore_signal(
                barrier, inc=1, device_id={"space": lax.rem(here + k, spaces)}, device_id_type=MESH
            )
            count += 1
    pl.semaphore_wait(barrier, count)


def propagate_kernel(
    peers,
    spaces,
    chunk,
    field_ref,
    wave_ref,
    substeps_ref,
    trig_ref,
    east_ref,
    north_ref,
    neighbour_ref,
    points_ref,
    states,
    speed_x,
    speed_y,
    repeats,
    selector,
    load_sem,
    halo_send,
    halo_recv,
    piece_send,
    piece_recv,
    own_sem,
):
    me = lax.axis_index("comp")
    here = lax.axis_index("space")
    rows, width = field_ref.shape
    tiles = width // HALO
    chunks = rows // chunk
    has_left = here > 0
    has_right = here < spaces - 1

    loads = [
        pltpu.make_async_copy(
            field_ref.at[:, pl.ds(j * HALO, HALO)], states.at[0, j + 1], load_sem.at[j]
        )
        for j in range(tiles)
    ]
    for load in loads:
        load.start()

    @pl.when(jnp.logical_not(has_left))
    def _():
        for s in range(SUB):
            states[s, 0] = jnp.zeros((rows, HALO), jnp.float32)

    @pl.when(jnp.logical_not(has_right))
    def _():
        for s in range(SUB):
            states[s, tiles + 1] = jnp.zeros((rows, HALO), jnp.float32)

    sync(peers, spaces)

    def halo_copies(s, first, count):
        part = pl.ds(first, count)
        chunk_id = first // chunk
        to_left = pltpu.make_async_remote_copy(
            src_ref=states.at[s, 1, part],
            dst_ref=states.at[s, tiles + 1, part],
            send_sem=halo_send.at[s, 0],
            recv_sem=halo_recv.at[s, 0, chunk_id],
            device_id={"space": jnp.maximum(here - 1, 0)},
            device_id_type=MESH,
        )
        to_right = pltpu.make_async_remote_copy(
            src_ref=states.at[s, tiles, part],
            dst_ref=states.at[s, 0, part],
            send_sem=halo_send.at[s, 1],
            recv_sem=halo_recv.at[s, 1, chunk_id],
            device_id={"space": jnp.minimum(here + 1, spaces - 1)},
            device_id_type=MESH,
        )
        return to_left, to_right

    def send_halo(s, c):
        to_left, to_right = halo_copies(s, c * chunk, chunk)

        @pl.when(has_left)
        def _():
            to_left.start()

        @pl.when(has_right)
        def _():
            to_right.start()

    def wait_halo(s, c):
        to_left, to_right = halo_copies(s, c * chunk, chunk)

        @pl.when(has_right)
        def _():
            to_left.wait_recv()

        @pl.when(has_left)
        def _():
            to_right.wait_recv()

    def piece(k, first, count):
        target = lax.rem(me + k, peers)
        return pltpu.make_async_remote_copy(
            src_ref=states.at[SUB, target + 1, pl.ds(first, count)],
            dst_ref=points_ref.at[pl.ds(pl.multiple_of(me * rows + first, 8), count)],
            send_sem=piece_send.at[k],
            recv_sem=piece_recv.at[k],
            device_id={"comp": target},
            device_id_type=MESH,
        )

    order = sorted(range(1, peers), key=lambda k: abs(k - peers / 2))

    def send_pieces(c):
        for k in order:
            piece(k, c * chunk, chunk).start()

    def lanes(j):
        return pl.ds(pl.multiple_of(j * HALO, HALO), HALO)

    sublane = lax.broadcasted_iota(jnp.int32, (8, HALO), 0)

    def prepare(c):
        def per_group(g, carry):
            row = pl.multiple_of(c * chunk + g * 8, 8)
            at = pl.ds(row, 8)
            component = me * rows + row
            speed = wave_ref[component // ND]
            turn = pl.ds(pl.multiple_of(lax.rem(component, ND), 8), 8)
            own_x = trig_ref[0, turn, :] * speed
            own_y = trig_ref[1, turn, :] * speed
            taken = jnp.full((8, HALO), substeps_ref[component], jnp.int32)
            for i in range(1, 8):
                taken = jnp.where(sublane == i, substeps_ref[component + i], taken)
            count = taken.astype(jnp.float32)
            repeats[at] = count
            scale = courant_scale / count

            def per_tile(j, inner):
                along_x = (own_x + east_ref[0:1, lanes(j)]) * scale
                along_y = (own_y + north_ref[0:1, lanes(j)]) * scale
                speed_x[j, at] = jnp.clip(along_x, -courant_limit, courant_limit)
                speed_y[j, at] = jnp.clip(along_y, -courant_limit, courant_limit)
                return inner

            return lax.fori_loop(0, tiles, per_tile, carry, unroll=tiles <= 4)

        lax.fori_loop(0, chunk // 8, per_group, 0)

    def choices(j, carry):
        spot = lax.broadcasted_iota(jnp.int32, (2 * HALO, HALO), 0)
        for d in range(4):
            wanted = neighbour_ref[d : d + 1, lanes(j)] - (j + d % 2) * HALO
            chosen = jnp.where(spot == wanted, 1.0, 0.0).astype(jnp.bfloat16)
            half = d // 2 * HALO
            selector[j, d % 2, :, half : half + HALO] = chosen
        return carry

    def split(x):
        high = x.astype(jnp.bfloat16)
        rest = x - high.astype(jnp.float32)
        middle = rest.astype(jnp.bfloat16)
        low = (rest - middle.astype(jnp.float32)).astype(jnp.bfloat16)
        return high, middle, low

    def pick(first, second, chosen):
        pairs = [jnp.concatenate(pair, axis=1) for pair in zip(first, second)]
        if chunk % 16 == 0:
            taken = jnp.dot(
                jnp.concatenate(pairs, axis=0), chosen, preferred_element_type=jnp.float32
            )
            terms = [taken[i * chunk : (i + 1) * chunk] for i in range(3)]
        else:
            terms = [jnp.dot(p, chosen, preferred_element_type=jnp.float32) for p in pairs]
        taken = terms[0] + terms[1] + terms[2]
        return taken[:, :HALO], taken[:, HALO:]

    def advance(s, c):
        at = pl.ds(c * chunk, chunk)

        def per_tile(j, carry):
            value = states[s, j + 1, at]
            here_split = split(value)
            west, south = pick(split(states[s, j, at]), here_split, selector[j, 0])
            east, north = pick(here_split, split(states[s, j + 2, at]), selector[j, 1])
            along_x = speed_x[j, at]
            along_y = speed_y[j, at]
            change = jnp.abs(along_x) * (value - jnp.where(along_x > 0.0, west, east))
            change = change + jnp.abs(along_y) * (value - jnp.where(along_y > 0.0, south, north))
            if s > 0:
                change = jnp.where(repeats[at] > float(s), change, 0.0)
            states[s + 1, j + 1, at] = value - change
            return carry

        lax.fori_loop(0, tiles, per_tile, 0, unroll=4)

    for load in loads:
        load.wait()
    for c in range(chunks):
        send_halo(0, c)
    lax.fori_loop(0, tiles, choices, 0)
    for wave in range(chunks + SKEW * (SUB - 1)):
        for s in reversed(range(SUB)):
            c = wave - SKEW * s
            if not 0 <= c < chunks:
                continue
            if s == 0:
                prepare(c)
            wait_halo(s, c)
            advance(s, c)
            if s + 1 < SUB:
                send_halo(s + 1, c)
            else:
                send_pieces(c)
    own = pltpu.make_async_copy(
        states.at[SUB, me + 1],
        points_ref.at[pl.ds(pl.multiple_of(me * rows, 8), rows)],
        own_sem,
    )
    own.start()
    own.wait()
    for s in range(SUB):
        to_left, to_right = halo_copies(s, 0, rows)

        @pl.when(has_left)
        def _():
            to_left.wait_send()

        @pl.when(has_right)
        def _():
            to_right.wait_send()

    for k in range(1, peers):
        whole = piece(k, 0, rows)
        whole.wait_send()
        whole.wait_recv()


def propagate(field, wave_speed, substeps, east, north, neighbours, peers, spaces):
    rows, width = field.shape
    tiles = width // HALO
    chunk = chunk_rows(rows)
    angles = (np.arange(ND, dtype=np.float32) + np.float32(0.5)) * np.float32(2.0 * math.pi / ND)
    trig = np.stack([np.cos(angles), np.sin(angles)])
    trig = np.ascontiguousarray(np.broadcast_to(trig[:, :, None], (2, ND, HALO)))
    vmem = pl.BlockSpec(memory_space=pltpu.VMEM)
    smem = pl.BlockSpec(memory_space=pltpu.SMEM)
    return pl.pallas_call(
        functools.partial(propagate_kernel, peers, spaces, chunk),
        out_shape=jax.ShapeDtypeStruct((peers * rows, HALO), jnp.float32),
        in_specs=[pl.BlockSpec(memory_space=pl.ANY), smem, smem, vmem, vmem, vmem, vmem],
        out_specs=vmem,
        scratch_shapes=[
            pltpu.VMEM((SUB + 1, tiles + 2, rows, HALO), jnp.float32),
            pltpu.VMEM((tiles, rows, HALO), jnp.float32),
            pltpu.VMEM((tiles, rows, HALO), jnp.float32),
            pltpu.VMEM((rows, HALO), jnp.float32),
            pltpu.VMEM((tiles, 2, 2 * HALO, 2 * HALO), jnp.bfloat16),
            pltpu.SemaphoreType.DMA((tiles,)),
            pltpu.SemaphoreType.DMA((SUB, 2)),
            pltpu.SemaphoreType.DMA((SUB, 2, rows // chunk)),
            pltpu.SemaphoreType.DMA((peers,)),
            pltpu.SemaphoreType.DMA((peers,)),
            pltpu.SemaphoreType.DMA,
        ],
        compiler_params=pltpu.CompilerParams(collective_id=0, has_side_effects=True),
    )(
        field,
        wave_speed,
        substeps,
        jnp.asarray(trig),
        east.reshape(1, width),
        north.reshape(1, width),
        neighbours,
    )


def source_kernel(batch, quad_ref, strength_ref, points_ref, blocks_ref, out_ref, rounded, products):
    total = blocks_ref.shape[0]

    def fill(f, carry):
        value = points_ref[f]
        rounded[f] = value.astype(jnp.bfloat16)
        out_ref[f] = value
        return carry

    lax.fori_loop(0, NF, fill, 0, unroll=4)

    def step(i, carry):
        for b in range(batch):
            j = i * batch + b
            block = blocks_ref[j]
            left = jnp.dot(block, rounded[quad_ref[0, j]], preferred_element_type=jnp.float32)
            right = lax.dot_general(
                block,
                rounded[quad_ref[1, j]],
                (((0,), (0,)), ((), ())),
                preferred_element_type=jnp.float32,
            )
            products[b] = (left * right * points_ref[quad_ref[2, j]]).astype(jnp.bfloat16)
        parts = []
        for b in range(batch):
            j = i * batch + b
            part = jnp.dot(blocks_ref[j], products[b], preferred_element_type=jnp.float32)
            parts.append(part * (strength_ref[j] * source_step))
        for b in range(batch):
            target = quad_ref[3, i * batch + b]
            out_ref[target] = out_ref[target] + parts[b]
        return carry

    lax.fori_loop(0, total // batch, step, 0)


def source_term(points, blocks, quad_index, strength):
    width = points.shape[1]
    vmem = pl.BlockSpec(memory_space=pltpu.VMEM)
    smem = pl.BlockSpec(memory_space=pltpu.SMEM)
    batch = math.gcd(blocks.shape[0], 32)
    out = pl.pallas_call(
        functools.partial(source_kernel, batch),
        out_shape=jax.ShapeDtypeStruct((NF, ND, width), jnp.float32),
        in_specs=[smem, smem, vmem, vmem],
        out_specs=vmem,
        scratch_shapes=[
            pltpu.VMEM((NF, ND, width), jnp.bfloat16),
            pltpu.VMEM((batch, ND, width), jnp.bfloat16),
        ],
    )(quad_index, strength, points.reshape(NF, ND, width), blocks)
    return out.reshape(NF * ND, width)


def home_kernel(peers, points_ref, out_ref, send_sem, recv_sem, own_sem):
    me = lax.axis_index("comp")
    rows = out_ref.shape[0]
    place = pl.ds(pl.multiple_of(me * HALO, HALO), HALO)
    own = pltpu.make_async_copy(
        points_ref.at[pl.ds(pl.multiple_of(me * rows, 8), rows)], out_ref.at[:, place], own_sem
    )
    own.start()
    sync(peers, 0)
    copies = []
    for k in sorted(range(1, peers), key=lambda k: abs(k - peers / 2)):
        target = lax.rem(me + k, peers)
        copy = pltpu.make_async_remote_copy(
            src_ref=points_ref.at[pl.ds(pl.multiple_of(target * rows, 8), rows)],
            dst_ref=out_ref.at[:, place],
            send_sem=send_sem.at[k],
            recv_sem=recv_sem.at[k],
            device_id={"comp": target},
            device_id_type=MESH,
        )
        copy.start()
        copies.append(copy)
    own.wait()
    for copy in copies:
        copy.wait()


def send_home(points, peers):
    rows = points.shape[0] // peers
    return pl.pallas_call(
        functools.partial(home_kernel, peers),
        out_shape=jax.ShapeDtypeStruct((rows, peers * HALO), jnp.float32),
        in_specs=[pl.BlockSpec(memory_space=pltpu.VMEM)],
        out_specs=pl.BlockSpec(memory_space=pltpu.VMEM),
        scratch_shapes=[
            pltpu.SemaphoreType.DMA((peers,)),
            pltpu.SemaphoreType.DMA((peers,)),
            pltpu.SemaphoreType.DMA,
        ],
        compiler_params=pltpu.CompilerParams(collective_id=1, has_side_effects=True),
    )(points)


def shards(
    spectrum,
    wave_speed,
    current_east,
    current_north,
    substeps,
    neighbours,
    blocks,
    quad_index,
    strength,
):
    peers = lax.axis_size("comp")
    spaces = lax.axis_size("space")
    rows, width = spectrum.shape
    assert width == peers * HALO
    points = propagate(
        spectrum, wave_speed, substeps, current_east, current_north, neighbours, peers, spaces
    )
    points = source_term(points, blocks, quad_index, strength)
    return send_home(points, peers)


def solution(mesh):
    in_specs = (
        P("comp", ("grp", "space")),
        P(),
        P(("grp", "space")),
        P(("grp", "space")),
        P(),
        P(None, ("grp", "space")),
        P(),
        P(),
        P(),
    )
    out_specs = P("comp", ("grp", "space"))
    return jax.shard_map(shards, mesh=mesh, in_specs=in_specs, out_specs=out_specs, check_vma=False)
```
